32 devices in a mesh: lat: 4 (over y, x), lon: 8 (over z, core).
Axes of the slice: x: 2, y: 2, z: 4, core: 2. Of those that a mesh axis runs over, the one named last changes fastest.
Arguments:
- tracer: float32 [1152, 512, 128], P('lon', 'lat'), may hold values from -6 to 6
- courant: float32 [2, 1152, 512, 128], P(None, 'lon', 'lat'), may hold values from -0.45 to 0.45
- polar_mask: int32 [512], replicated, may hold values from 0 to 1, as said below
- cutoff: int32 [512], replicated, may hold values from 2 to 576
Outputs:
- advected: float32 [1152, 512, 128], P('lon', 'lat')
The draws below stay inside these ranges and needn't reach their ends.
Inputs may be any that keep to these rules, and one draw needn't show every extreme that they name: polar_mask is 1 on the first a rows and on the last b rows, with a and b each between 64 and 256, and 0 on all other rows.
All inputs are finite; a program needn't handle non-finite values.
Results may differ from the reference program's by a relative error of at most 0.00007.
Values sent between devices are 32-bit elements; how exact they have to be, the bound alone decides.
A program may use at most 256 MiB of HBM per device.

```python
import jax
import jax.numpy as jnp
from jax import lax

NLON = 1152
CLAT = 128
NF = 128
NLAT = 512


def draw_polar_mask(key, part):
    north_depth = jax.random.randint(jax.random.fold_in(key, 101), (), CLAT // 2, 2 * CLAT + 1)
    south_depth = jax.random.randint(jax.random.fold_in(key, 202), (), CLAT // 2, 2 * CLAT + 1)
    rows = jnp.arange(NLAT, dtype=jnp.int32)
    north = rows < north_depth
    south = rows >= NLAT - south_depth
    return jnp.where(north | south, 1, 0).astype(jnp.int32)


def place_ends(values, rng, least, top_value):
    longest = values.shape.index(max(values.shape))
    spots = []
    for shift in (0, 1):
        where = [jax.random.randint(jax.random.fold_in(rng, axis), (), 0, length) for axis, length in enumerate(values.shape)]
        where[longest] = (where[longest] + shift) % values.shape[longest]
        spots.append(tuple(where))
    return values.at[spots[0]].set(least).at[spots[1]].set(top_value)


def level_of(rng, dims, pieces, least, top_value):
    loudness = 1.0
    for position, blocks in pieces:
        heights = jax.random.uniform(jax.random.fold_in(jax.random.fold_in(rng, 6), position), (blocks,), jnp.float32, least / len(pieces), top_value / len(pieces))
        loudness = loudness * jnp.repeat(jnp.exp(heights), dims[position] // blocks).reshape((-1,) + (1,) * (len(dims) - 1 - position))
    return loudness


def normal_values(key, dims, spread, bound, shards=(), kind=jnp.bfloat16):
    entries = spread * jax.random.normal(key, dims, jnp.float32)
    if shards:
        entries = entries * level_of(key, dims, shards, -0.22, 0.18)
    return jnp.clip(entries, -bound, bound).astype(kind)


def setup_inputs(seed: int = 0) -> dict:
    key_list = jax.random.split(jax.random.key(seed), 5)
    return {
        "tracer": normal_values(key_list[0], (NLON, NLAT, NF), 1.0, 6.0, ((0, 8), (1, 4)), jnp.float32),
        "courant": jnp.clip(jax.random.uniform(key_list[1], (2, NLON, NLAT, NF), jnp.float32, -0.45, 0.45) * level_of(key_list[1], (2, NLON, NLAT, NF), ((1, 8), (2, 4)), -0.4, 0.0), -0.45, 0.45),
        "polar_mask": draw_polar_mask(jax.random.fold_in(key_list[4], 71), 0),
        "cutoff": place_ends(jax.random.randint(key_list[3], (NLAT,), 2, NLON // 2 + 1), jax.random.fold_in(key_list[3], 1), 2, (NLON // 2 + 1) - 1).astype(jnp.int32),
    }


def flux_change(padded_field, padded_speed, axis, count):
    def part(array, first):
        return lax.slice_in_dim(array, first, first + count + 1, axis=axis)
    far_low = part(padded_field, 0)
    low = part(padded_field, 1)
    high = part(padded_field, 2)
    far_high = part(padded_field, 3)
    speed = part(padded_speed, 2)
    face = (7.0 / 12.0) * (low + high) - (1.0 / 12.0) * (far_low + far_high)
    limited = jnp.clip(face, jnp.minimum(low, high), jnp.maximum(low, high))
    flux = speed * limited
    return lax.slice_in_dim(flux, 1, count + 1, axis=axis) - lax.slice_in_dim(flux, 0, count, axis=axis)


def reference(tracer, courant, polar_mask, cutoff):
    nlon, nlat, nf = tracer.shape
    blocks = 8
    width = nf // blocks

    def one_block(items):
        field, speed_x, speed_y = items
        spectrum = jnp.fft.rfft(field, axis=0)
        keep = (jnp.arange(nlon // 2 + 1, dtype=jnp.int32)[:, None] < cutoff[None, :]).astype(field.dtype)
        smooth = jnp.fft.irfft(spectrum * keep[:, :, None], n=nlon, axis=0).astype(field.dtype)
        weight = polar_mask.astype(field.dtype)[None, :, None]
        filtered = field + weight * (smooth - field)
        wide_field = jnp.pad(filtered, ((2, 2), (0, 0), (0, 0)), mode="wrap")
        wide_speed = jnp.pad(speed_x, ((2, 2), (0, 0), (0, 0)), mode="wrap")
        tall_field = jnp.pad(filtered, ((0, 0), (2, 2), (0, 0)))
        tall_speed = jnp.pad(speed_y, ((0, 0), (2, 2), (0, 0)))
        change_x = flux_change(wide_field, wide_speed, 0, nlon)
        change_y = flux_change(tall_field, tall_speed, 1, nlat)
        return filtered - change_x - change_y

    def split(array):
        return array.reshape(nlon, nlat, blocks, width).transpose(2, 0, 1, 3)

    result = lax.map(one_block, (split(tracer), split(courant[0]), split(courant[1])))
    return result.transpose(1, 2, 0, 3).reshape(nlon, nlat, nf)
```

```python
import functools
import math

import jax
import jax.numpy as jnp
import ml_dtypes
import numpy as np
from jax import lax
from jax.experimental import pallas as pl
from jax.experimental.pallas import tpu as pltpu
from jax.sharding import PartitionSpec as P

MESH = pl.DeviceIdType.MESH


def halves(table):
    high = table.astype(ml_dtypes.bfloat16)
    low = (table - high.astype(np.float64)).astype(ml_dtypes.bfloat16)
    return high, low


def hartley_tables(nlon):
    half = nlon // 2
    u = np.arange(half, dtype=np.int64)
    even = (u[:, None] * u[None, :]) % half * (2.0 * math.pi / half)
    odd = ((2 * u[:, None] + 1) * (2 * u[None, :] + 1)) % (2 * nlon) * (math.pi / nlon)
    cas = lambda t: np.cos(t) + np.sin(t)
    return (*halves(cas(even)), *halves(cas(odd)))


def split(x):
    high = x.astype(jnp.bfloat16)
    return high, (x - high.astype(jnp.float32)).astype(jnp.bfloat16)


def times(high, low, x):
    x_high, x_low = split(x)
    dot = functools.partial(jnp.dot, preferred_element_type=jnp.float32)
    return dot(high[...], x_high) + (dot(low[...], x_high) + dot(high[...], x_low))


def filter_kernel(devices, chunks, mask_ref, cut_ref, even_h, even_l, odd_h, odd_l, tracer, out,
                  ring, send_a, recv_a, self_a, send_b, recv_b, self_b):
    me = lax.axis_index("lon")
    clon, clat, nf = tracer.shape
    rows = clat // devices
    size = rows // chunks
    nlon = clon * devices
    half = nlon // 2
    first_row = lax.axis_index("lat") * clat + me * rows
    peers = [lax.rem(me + off, devices) for off in range(1, devices)]

    barrier = pltpu.get_barrier_semaphore()
    for peer in peers:
        pl.semaphore_signal(barrier, inc=1, device_id={"lon": peer}, device_id_type=MESH)
    pl.semaphore_wait(barrier, devices - 1)

    def source(owner, c):
        return tracer.at[:, pl.ds(pl.multiple_of(owner * rows + c * size, size), size), :]

    def landing(c):
        return ring.at[c, pl.ds(2 + me * clon, clon)]

    def result(owner, c):
        return ring.at[c, pl.ds(owner * clon, clon + 4)]

    def home(c):
        return out.at[:, pl.ds(pl.multiple_of(me * rows + c * size, size), size), :]

    there, back = [], []
    for c in range(chunks):
        own = pltpu.make_async_copy(source(me, c), landing(c), self_a.at[c])
        sent = [
            pltpu.make_async_remote_copy(
                source(peer, c), landing(c), send_a.at[c, j], recv_a.at[c, j],
                device_id={"lon": peer}, device_id_type=MESH)
            for j, peer in enumerate(peers)
        ]
        own.start()
        for copy in sent:
            copy.start()
        there.append((own, sent))

    lane = lax.broadcasted_iota(jnp.int32, (1, 2 * nf), 1)
    index = lax.broadcasted_iota(jnp.int32, (half, 2 * nf), 0)
    scale = 1.0 / nlon

    for c in range(chunks):
        own, sent = there[c]
        own.wait()
        for copy in sent:
            copy.wait_recv()
        flat = ring.at[c].reshape((nlon + 4) * size, nf)

        def pair(p, carry):
            def block(start, count, r):
                return (pl.ds(start * size + r, count, stride=size), slice(None))

            def load(start):
                return jnp.concatenate(
                    [flat[block(start, half, 2 * p + s)] for s in range(2)], axis=1)

            row = first_row + c * size + 2 * p
            cut = jnp.where(lane < nf, cut_ref[row], cut_ref[row + 1])
            mask = jnp.where(lane < nf, mask_ref[row], mask_ref[row + 1])
            low, high = load(2), load(2 + half)
            even = times(even_h, even_l, low + high)
            odd = times(odd_h, odd_l, low - high)
            wave = 2 * index
            even = jnp.where(jnp.minimum(wave, nlon - wave) < cut, even * scale, 0.0)
            odd = jnp.where(jnp.minimum(wave + 1, nlon - 1 - wave) < cut, odd * scale, 0.0)
            even = times(even_h, even_l, even)
            odd = times(odd_h, odd_l, odd)
            low = jnp.where(mask > 0, even + odd, low)
            high = jnp.where(mask > 0, even - odd, high)
            for s in range(2):
                r = 2 * p + s
                lo, hi = low[:, s * nf:(s + 1) * nf], high[:, s * nf:(s + 1) * nf]
                flat[block(2, half, r)] = lo
                flat[block(2 + half, half, r)] = hi
                for e in range(2):
                    flat[pl.ds((2 + nlon + e) * size + r, 1), :] = lo[e:e + 1]
                    flat[pl.ds(e * size + r, 1), :] = hi[half - 2 + e:half - 1 + e]
            return carry

        lax.fori_loop(0, size // 2, pair, 0)

        own = pltpu.make_async_copy(result(me, c), home(c), self_b.at[c])
        sent = [
            pltpu.make_async_remote_copy(
                result(peer, c), home(c), send_b.at[c, j], recv_b.at[c, j],
                device_id={"lon": peer}, device_id_type=MESH)
            for j, peer in enumerate(peers)
        ]
        own.start()
        for copy in sent:
            copy.start()
        back.append((own, sent))

    for c in range(chunks):
        for copy in there[c][1]:
            copy.wait_send()
        own, sent = back[c]
        own.wait()
        for copy in sent:
            copy.wait()


def filtered_columns(tracer, polar_mask, cutoff, devices):
    clon, clat, nf = tracer.shape
    nlon = clon * devices
    rows = clat // devices
    chunks = rows // 8
    size = rows // chunks
    tables = [jnp.asarray(t) for t in hartley_tables(nlon)]
    smem = pl.BlockSpec(memory_space=pltpu.SMEM)
    vmem = pl.BlockSpec(memory_space=pltpu.VMEM)
    hbm = pl.BlockSpec(memory_space=pl.ANY)
    pairs = pltpu.SemaphoreType.DMA((chunks, devices - 1))
    alone = pltpu.SemaphoreType.DMA((chunks,))
    return pl.pallas_call(
        functools.partial(filter_kernel, devices, chunks),
        out_shape=jax.ShapeDtypeStruct((clon + 4, clat, nf), jnp.float32),
        in_specs=[smem, smem, vmem, vmem, vmem, vmem, hbm],
        out_specs=hbm,
        scratch_shapes=[pltpu.VMEM((chunks, nlon + 4, size, nf), jnp.float32),
                        pairs, pairs, alone, pairs, pairs, alone],
        compiler_params=pltpu.CompilerParams(
            collective_id=0, has_side_effects=True, vmem_limit_bytes=48 << 20),
        name="filter_exchange",
    )(polar_mask, cutoff, *tables, tracer)


def limited(far_low, low, high, far_high):
    face = (7.0 / 12.0) * (low + high) - (1.0 / 12.0) * (far_low + far_high)
    return jnp.minimum(jnp.maximum(face, jnp.minimum(low, high)), jnp.maximum(low, high))


def flux_kernel(field, speed_x, next_x, edge_x, speed_y, edge_y, before, after, out, tall, flux):
    count, clat = out.shape[0], out.shape[1]
    final = pl.program_id(0) == pl.num_programs(0) - 1

    def flux_x(i, speed):
        return speed * limited(field[i], field[i + 1], field[i + 2], field[i + 3])

    def column(c, low_flux, speed):
        high_flux = flux_x(c + 1, speed)
        value = field[c + 2]
        tall[8:8 + clat] = value
        tall[6:8] = before[c]
        tall[8 + clat:10 + clat] = after[c]
        flux[0:clat] = speed_y[c] * limited(
            tall[6:6 + clat], tall[7:7 + clat], value, tall[9:9 + clat])
        flux[clat:clat + 1] = edge_y[c] * limited(
            tall[6 + clat:7 + clat], tall[7 + clat:8 + clat],
            tall[8 + clat:9 + clat], tall[9 + clat:10 + clat])
        out[c] = value - (high_flux - low_flux) - (flux[1:clat + 1] - flux[0:clat])
        return high_flux

    carry = flux_x(0, speed_x[0])
    carry = lax.fori_loop(0, count - 1, lambda c, low: column(c, low, speed_x[c + 1]), carry)
    column(count - 1, carry, jnp.where(final, edge_x[0], next_x[0]))


def advect(field, courant, edge_x, edge_y, before, after):
    _, clon, clat, nf = courant.shape
    block = math.gcd(clon, 16)
    squeezed = pl.Squeezed()
    return pl.pallas_call(
        flux_kernel,
        grid=(clon // block,),
        out_shape=jax.ShapeDtypeStruct((clon, clat, nf), jnp.float32),
        in_specs=[
            pl.BlockSpec((pl.Element(block + 4), pl.Element(clat), pl.Element(nf)),
                         lambda i: (i * block, 0, 0)),
            pl.BlockSpec((squeezed, block, clat, nf), lambda i: (0, i, 0, 0)),
            pl.BlockSpec((squeezed, 1, clat, nf),
                         lambda i: (0, jnp.minimum((i + 1) * block, clon - 1), 0, 0)),
            pl.BlockSpec((1, clat, nf), lambda i: (0, 0, 0)),
            pl.BlockSpec((squeezed, block, clat, nf), lambda i: (1, i, 0, 0)),
            pl.BlockSpec((block, 1, nf), lambda i: (i, 0, 0)),
            pl.BlockSpec((block, 2, nf), lambda i: (i, 0, 0)),
            pl.BlockSpec((block, 2, nf), lambda i: (i, 0, 0)),
        ],
        out_specs=pl.BlockSpec((block, clat, nf), lambda i: (i, 0, 0)),
        scratch_shapes=[pltpu.VMEM((clat + 16, nf), jnp.float32),
                        pltpu.VMEM((clat + 8, nf), jnp.float32)],
        compiler_params=pltpu.CompilerParams(vmem_limit_bytes=48 << 20),
        name="flux_step",
    )(field, courant, courant, edge_x, courant, edge_y, before, after)


def filtered_by_collectives(tracer, polar_mask, cutoff, devices):
    clon, clat, nf = tracer.shape
    nlon, half = clon * devices, clon * devices // 2
    circles = lax.all_to_all(tracer, "lon", split_axis=1, concat_axis=0, tiled=True)
    rows = clat // devices
    start = lax.axis_index("lat") * clat + lax.axis_index("lon") * rows
    mask = lax.dynamic_slice_in_dim(polar_mask, start, rows)[None, :, None]
    cut = lax.dynamic_slice_in_dim(cutoff, start, rows)[None, :, None]
    tables = [jnp.asarray(t).astype(jnp.float32) for t in hartley_tables(nlon)]
    apply = lambda h, l, x: jnp.einsum("uk,krc->urc", h + l, x, precision=lax.Precision.HIGHEST)
    low, high = circles[:half], circles[half:]
    wave = 2 * lax.broadcasted_iota(jnp.int32, (half, 1, 1), 0)
    even = apply(tables[0], tables[1], low + high) * (1.0 / nlon)
    odd = apply(tables[2], tables[3], low - high) * (1.0 / nlon)
    even = jnp.where(jnp.minimum(wave, nlon - wave) < cut, even, 0.0)
    odd = jnp.where(jnp.minimum(wave + 1, nlon - 1 - wave) < cut, odd, 0.0)
    even = apply(tables[0], tables[1], even)
    odd = apply(tables[2], tables[3], odd)
    smooth = jnp.concatenate([even + odd, even - odd], axis=0)
    done = jnp.where(mask > 0, smooth, circles)
    field = lax.all_to_all(done, "lon", split_axis=0, concat_axis=1, tiled=True)
    up = [(i, (i + 1) % devices) for i in range(devices)]
    down = [(j, i) for i, j in up]
    before = lax.ppermute(field[clon - 2:], "lon", up)
    after = lax.ppermute(field[:2], "lon", down)
    return jnp.concatenate([before, field, after], axis=0)


def on_device(tracer, courant, polar_mask, cutoff):
    clon, clat, nf = tracer.shape
    devices, bands = lax.axis_size("lon"), lax.axis_size("lat")
    west = [((i + 1) % devices, i) for i in range(devices)]
    south = [(i, i + 1) for i in range(bands - 1)]
    north = [(j, i) for i, j in south]
    edge_x = lax.ppermute(courant[0, :1], "lon", west)
    edge_y = lax.ppermute(courant[1, :, :1], "lat", north)
    whole = clat % (8 * devices) == 0
    build = filtered_columns if whole else filtered_by_collectives
    field = build(tracer, polar_mask, cutoff, devices)
    before = lax.ppermute(field[2:2 + clon, clat - 2:], "lat", south)
    after = lax.ppermute(field[2:2 + clon, :2], "lat", north)
    return advect(field, courant, edge_x, edge_y, before, after)


def solution(mesh):
    return jax.shard_map(
        on_device,
        mesh=mesh,
        in_specs=(P("lon", "lat", None), P(None, "lon", "lat", None), P(), P()),
        out_specs=P("lon", "lat", None),
        check_vma=False,
    )
```

```python
import functools
import math

import jax
import jax.numpy as jnp
import ml_dtypes
import numpy as np
from jax import lax
from jax.experimental import pallas as pl
from jax.experimental.pallas import tpu as pltpu
from jax.sharding import PartitionSpec as P

MESH = pl.DeviceIdType.MESH


def halves(table):
    high = table.astype(ml_dtypes.bfloat16)
    low = (table - high.astype(np.float64)).astype(ml_dtypes.bfloat16)
    return high, low


def hartley_tables(nlon):
    half = nlon // 2
    u = np.arange(half, dtype=np.int64)
    even = (u[:, None] * u[None, :]) % half * (2.0 * math.pi / half)
    odd = ((2 * u[:, None] + 1) * (2 * u[None, :] + 1)) % (2 * nlon) * (math.pi / nlon)
    cas = lambda t: np.cos(t) + np.sin(t)
    return (*halves(cas(even)), *halves(cas(odd)))


def split(x):
    high = x.astype(jnp.bfloat16)
    return high, (x - high.astype(jnp.float32)).astype(jnp.bfloat16)


def times(high, low, x):
    x_high, x_low = split(x)
    dot = functools.partial(jnp.dot, preferred_element_type=jnp.float32)
    return dot(high[...], x_high) + (dot(low[...], x_high) + dot(high[...], x_low))


def filter_kernel(devices, bands, chunks, mask_ref, cut_ref, tracer, courant, *rest):
    tables, rest = rest[:4], rest[4:]
    (out, before, after, edge_x, edge_y, ring, even_h, even_l, odd_h, odd_l,
     table_sem, send_a, recv_a, self_a, send_b, recv_b, self_b, send_e, recv_e) = rest
    me, lat = lax.axis_index("lon"), lax.axis_index("lat")
    clon, clat, nf = tracer.shape
    size = clat // devices // chunks
    nlon = clon * devices
    half = nlon // 2
    order = sorted(range(1, devices), key=lambda off: -min(off, devices - off))
    peers = [lax.rem(me + off, devices) for off in order]
    west = lax.rem(me + devices - 1, devices)
    north, south = lax.rem(lat + bands - 1, bands), lax.rem(lat + 1, bands)

    loads = [
        pltpu.make_async_copy(table, place, table_sem.at[i])
        for i, (table, place) in enumerate(zip(tables, (even_h, even_l, odd_h, odd_l)))
    ]
    for copy in loads:
        copy.start()

    barrier = pltpu.get_barrier_semaphore()
    for peer in peers:
        pl.semaphore_signal(barrier, inc=1, device_id={"lon": peer}, device_id_type=MESH)
    for band in (north, south):
        pl.semaphore_signal(barrier, inc=1, device_id={"lat": band}, device_id_type=MESH)
    pl.semaphore_wait(barrier, devices + 1)

    def first(owner, c):
        flip = owner // (devices // 2)
        tile = owner * chunks + c + flip * (chunks - 1 - 2 * c)
        return pl.multiple_of(tile * size, size)

    def landing(c):
        return ring.at[c, pl.ds(2 + me * clon, clon)]

    def result(owner, c):
        return ring.at[c, pl.ds(owner * clon, clon + 4)]

    def home(c):
        return out.at[:, pl.ds(first(me, c), size), :]

    def source(owner, c):
        return tracer.at[:, pl.ds(first(owner, c), size), :]

    there, back = [], []
    for c in range(chunks):
        own = pltpu.make_async_copy(source(me, c), landing(c), self_a.at[c])
        sent = [
            pltpu.make_async_remote_copy(
                source(peer, c), landing(c), send_a.at[c, j], recv_a.at[c, j],
                device_id={"lon": peer}, device_id_type=MESH)
            for j, peer in enumerate(peers)
        ]
        own.start()
        for j, copy in enumerate(sent):
            if c:
                there[-1][1][j].wait_send()
            copy.start()
        there.append((own, sent))

    def edge(src, dst, k, device):
        return pltpu.make_async_remote_copy(
            src, dst, send_e.at[k], recv_e.at[k], device_id=device, device_id_type=MESH)

    def inner(ref, start):
        return ref.at[pl.ds(2, clon), pl.ds(start, 8), :]

    go_x = edge(courant.at[0, pl.ds(0, 1)], edge_x, 0, {"lon": west})
    go_y = edge(courant.at[1, :, pl.ds(0, 8), :], edge_y, 1, {"lat": north})
    go_north = edge(inner(out, 0), after, 2, {"lat": north})
    go_south = edge(inner(out, clat - 8), before, 3, {"lat": south})
    go_x.start()
    go_y.start()
    for copy in loads:
        copy.wait()

    lane = lax.broadcasted_iota(jnp.int32, (1, 2 * nf), 1)
    index = lax.broadcasted_iota(jnp.int32, (half, 2 * nf), 0)
    scale = 1.0 / nlon

    for c in range(chunks):
        own, sent = there[c]
        own.wait()
        for copy in sent:
            copy.wait_recv()
        flat = ring.at[c].reshape((nlon + 4) * size, nf)
        first_row = lat * clat + first(me, c)

        def pair(p, carry):
            def block(start, count, r):
                return (pl.ds(start * size + r, count, stride=size), slice(None))

            def load(start):
                return jnp.concatenate(
                    [flat[block(start, half, 2 * p + s)] for s in range(2)], axis=1)

            row = first_row + 2 * p
            cut = jnp.where(lane < nf, cut_ref[row], cut_ref[row + 1])
            mask = jnp.where(lane < nf, mask_ref[row], mask_ref[row + 1])
            low, high = load(2), load(2 + half)
            even = times(even_h, even_l, low + high)
            odd = times(odd_h, odd_l, low - high)
            wave = 2 * index
            even = jnp.where(jnp.minimum(wave, nlon - wave) < cut, even * scale, 0.0)
            odd = jnp.where(jnp.minimum(wave + 1, nlon - 1 - wave) < cut, odd * scale, 0.0)
            even = times(even_h, even_l, even)
            odd = times(odd_h, odd_l, odd)
            low = jnp.where(mask > 0, even + odd, low)
            high = jnp.where(mask > 0, even - odd, high)
            for s in range(2):
                r = 2 * p + s
                lo, hi = low[:, s * nf:(s + 1) * nf], high[:, s * nf:(s + 1) * nf]
                flat[block(2, half, r)] = lo
                flat[block(2 + half, half, r)] = hi
                for e in range(2):
                    flat[pl.ds((2 + nlon + e) * size + r, 1), :] = lo[e:e + 1]
                    flat[pl.ds(e * size + r, 1), :] = hi[half - 2 + e:half - 1 + e]
            return carry

        lax.fori_loop(0, size // 2, pair, 0)

        own = pltpu.make_async_copy(result(me, c), home(c), self_b.at[c])
        sent = [
            pltpu.make_async_remote_copy(
                result(peer, c), home(c), send_b.at[c, j], recv_b.at[c, j],
                device_id={"lon": peer}, device_id_type=MESH)
            for j, peer in enumerate(peers)
        ]
        own.start()
        for copy in sent:
            copy.start()
        back.append((own, sent))

    for copy in there[-1][1]:
        copy.wait_send()
    go_x.wait()
    for c in range(chunks):
        own, sent = back[c]
        own.wait()
        for copy in sent:
            copy.wait()
        if c == 0:
            @pl.when(lat > 0)
            def _():
                go_north.start()

            @pl.when(lat < bands - 1)
            def _():
                go_south.start()
    go_y.wait()

    @pl.when(lat > 0)
    def _():
        go_north.wait_send()
        go_south.wait_recv()

    @pl.when(lat < bands - 1)
    def _():
        go_south.wait_send()
        go_north.wait_recv()


def by_kernel(tracer, courant, polar_mask, cutoff, devices, bands):
    clon, clat, nf = tracer.shape
    nlon = clon * devices
    half = nlon // 2
    chunks = clat // devices // 8
    tables = [jnp.asarray(t) for t in hartley_tables(nlon)]
    smem = pl.BlockSpec(memory_space=pltpu.SMEM)
    hbm = pl.BlockSpec(memory_space=pl.ANY)
    dma = pltpu.SemaphoreType.DMA
    pairs, alone = dma((chunks, devices - 1)), dma((chunks,))
    shape = lambda *dims: jax.ShapeDtypeStruct(dims, jnp.float32)
    edge = shape(clon, 8, nf)
    return pl.pallas_call(
        functools.partial(filter_kernel, devices, bands, chunks),
        out_shape=(shape(clon + 4, clat, nf), edge, edge, shape(1, clat, nf), edge),
        in_specs=[smem, smem] + [hbm] * 6,
        out_specs=(hbm,) * 5,
        scratch_shapes=[pltpu.VMEM((chunks, nlon + 4, 8, nf), jnp.float32)]
        + [pltpu.VMEM((half, half), jnp.bfloat16)] * 4
        + [dma((4,)), pairs, pairs, alone, pairs, pairs, alone, dma((4,)), dma((4,))],
        compiler_params=pltpu.CompilerParams(
            collective_id=0, has_side_effects=True, vmem_limit_bytes=48 << 20),
        name="filter_exchange",
    )(polar_mask, cutoff, tracer, courant, *tables)


def limited(far_low, low, high, far_high):
    face = (7.0 / 12.0) * (low + high) - (1.0 / 12.0) * (far_low + far_high)
    return jnp.minimum(jnp.maximum(face, jnp.minimum(low, high)), jnp.maximum(low, high))


def flux_kernel(bands, field, speed_x, next_x, edge_x, speed_y, edge_y, before, after, out, tall, flux):
    count, clat = out.shape[0], out.shape[1]
    final = pl.program_id(0) == pl.num_programs(0) - 1
    lat = lax.axis_index("lat")
    top, bottom = lat > 0, lat < bands - 1

    def flux_x(i, speed):
        return speed * limited(field[i], field[i + 1], field[i + 2], field[i + 3])

    def column(c, low_flux, speed):
        high_flux = flux_x(c + 1, speed)
        value = field[c + 2]
        tall[8:8 + clat] = value
        tall[0:8] = jnp.where(top, before[c], 0.0)
        tall[8 + clat:16 + clat] = jnp.where(bottom, after[c], 0.0)
        flux[0:clat] = speed_y[c] * limited(
            tall[6:6 + clat], tall[7:7 + clat], value, tall[9:9 + clat])
        flux[clat:clat + 1] = jnp.where(bottom, edge_y[c, 0:1], 0.0) * limited(
            tall[6 + clat:7 + clat], tall[7 + clat:8 + clat],
            tall[8 + clat:9 + clat], tall[9 + clat:10 + clat])
        out[c] = value - (high_flux - low_flux) - (flux[1:clat + 1] - flux[0:clat])
        return high_flux

    carry = flux_x(0, speed_x[0])
    carry = lax.fori_loop(0, count - 1, lambda c, low: column(c, low, speed_x[c + 1]), carry)
    column(count - 1, carry, jnp.where(final, edge_x[0], next_x[0]))


def advect(field, before, after, edge_x, edge_y, courant, bands):
    _, clon, clat, nf = courant.shape
    block = math.gcd(clon, 16)
    squeezed = pl.Squeezed()
    return pl.pallas_call(
        functools.partial(flux_kernel, bands),
        grid=(clon // block,),
        out_shape=jax.ShapeDtypeStruct((clon, clat, nf), jnp.float32),
        in_specs=[
            pl.BlockSpec((pl.Element(block + 4), pl.Element(clat), pl.Element(nf)),
                         lambda i: (i * block, 0, 0)),
            pl.BlockSpec((squeezed, block, clat, nf), lambda i: (0, i, 0, 0)),
            pl.BlockSpec((squeezed, 1, clat, nf),
                         lambda i: (0, jnp.minimum((i + 1) * block, clon - 1), 0, 0)),
            pl.BlockSpec((1, clat, nf), lambda i: (0, 0, 0)),
            pl.BlockSpec((squeezed, block, clat, nf), lambda i: (1, i, 0, 0)),
            pl.BlockSpec((block, 8, nf), lambda i: (i, 0, 0)),
            pl.BlockSpec((block, 8, nf), lambda i: (i, 0, 0)),
            pl.BlockSpec((block, 8, nf), lambda i: (i, 0, 0)),
        ],
        out_specs=pl.BlockSpec((block, clat, nf), lambda i: (i, 0, 0)),
        scratch_shapes=[pltpu.VMEM((clat + 16, nf), jnp.float32),
                        pltpu.VMEM((clat + 8, nf), jnp.float32)],
        compiler_params=pltpu.CompilerParams(vmem_limit_bytes=48 << 20),
        name="flux_step",
    )(field, courant, courant, edge_x, courant, edge_y, before, after)


def by_collectives(tracer, courant, polar_mask, cutoff, devices, bands):
    clon, clat, nf = tracer.shape
    nlon, half = clon * devices, clon * devices // 2
    circles = lax.all_to_all(tracer, "lon", split_axis=1, concat_axis=0, tiled=True)
    rows = clat // devices
    start = lax.axis_index("lat") * clat + lax.axis_index("lon") * rows
    mask = lax.dynamic_slice_in_dim(polar_mask, start, rows)[None, :, None]
    cut = lax.dynamic_slice_in_dim(cutoff, start, rows)[None, :, None]
    tables = [jnp.asarray(t).astype(jnp.float32) for t in hartley_tables(nlon)]
    apply = lambda h, l, x: jnp.einsum("uk,krc->urc", h + l, x, precision=lax.Precision.HIGHEST)
    low, high = circles[:half], circles[half:]
    wave = 2 * lax.broadcasted_iota(jnp.int32, (half, 1, 1), 0)
    even = apply(tables[0], tables[1], low + high) * (1.0 / nlon)
    odd = apply(tables[2], tables[3], low - high) * (1.0 / nlon)
    even = jnp.where(jnp.minimum(wave, nlon - wave) < cut, even, 0.0)
    odd = jnp.where(jnp.minimum(wave + 1, nlon - 1 - wave) < cut, odd, 0.0)
    even = apply(tables[0], tables[1], even)
    odd = apply(tables[2], tables[3], odd)
    smooth = jnp.concatenate([even + odd, even - odd], axis=0)
    done = jnp.where(mask > 0, smooth, circles)
    field = lax.all_to_all(done, "lon", split_axis=0, concat_axis=1, tiled=True)
    up = [(i, (i + 1) % devices) for i in range(devices)]
    down = [(j, i) for i, j in up]
    before = lax.ppermute(field[clon - 2:], "lon", up)
    after = lax.ppermute(field[:2], "lon", down)
    wide = jnp.concatenate([before, field, after], axis=0)
    south = [(i, i + 1) for i in range(bands - 1)]
    north = [(j, i) for i, j in south]
    edge_x = lax.ppermute(courant[0, :1], "lon", down)
    edge_y = lax.ppermute(courant[1, :, :8], "lat", north)
    before = lax.ppermute(field[:, clat - 8:], "lat", south)
    after = lax.ppermute(field[:, :8], "lat", north)
    return wide, before, after, edge_x, edge_y


def on_device(tracer, courant, polar_mask, cutoff):
    devices, bands = lax.axis_size("lon"), lax.axis_size("lat")
    fits = tracer.shape[1] % (8 * devices) == 0 and bands > 2
    build = by_kernel if fits else by_collectives
    parts = build(tracer, courant, polar_mask, cutoff, devices, bands)
    return advect(*parts, courant, bands)


def solution(mesh):
    return jax.shard_map(
        on_device,
        mesh=mesh,
        in_specs=(P("lon", "lat", None), P(None, "lon", "lat", None), P(), P()),
        out_specs=P("lon", "lat", None),
        check_vma=False,
    )
```

```python
import functools
import math

import jax
import jax.numpy as jnp
import ml_dtypes
import numpy as np
from jax import lax
from jax.experimental import pallas as pl
from jax.experimental.pallas import tpu as pltpu
from jax.sharding import PartitionSpec as P

MESH = pl.DeviceIdType.MESH


def halves(table):
    high = table.astype(ml_dtypes.bfloat16)
    low = (table - high.astype(np.float64)).astype(ml_dtypes.bfloat16)
    return high, low


def hartley_tables(nlon):
    half = nlon // 2
    u = np.arange(half, dtype=np.int64)
    even = (u[:, None] * u[None, :]) % half * (2.0 * math.pi / half)
    odd = ((2 * u[:, None] + 1) * (2 * u[None, :] + 1)) % (2 * nlon) * (math.pi / nlon)
    cas = lambda t: np.cos(t) + np.sin(t)
    return (*halves(cas(even)), *halves(cas(odd)))


def split(x):
    high = x.astype(jnp.bfloat16)
    return high, (x - high.astype(jnp.float32)).astype(jnp.bfloat16)


def times(high, low, x):
    x_high, x_low = split(x)
    dot = functools.partial(jnp.dot, preferred_element_type=jnp.float32)
    return dot(high[...], x_high) + (dot(low[...], x_high) + dot(high[...], x_low))


def filter_kernel(devices, bands, chunks, mask_ref, cut_ref, tracer, courant, *rest):
    tables, rest = rest[:4], rest[4:]
    (out, before, after, edge_x, edge_y, ring, even_h, even_l, odd_h, odd_l,
     table_sem, send_a, recv_a, self_a, send_b, recv_b, self_b, send_e, recv_e) = rest
    me, lat = lax.axis_index("lon"), lax.axis_index("lat")
    clon, clat, nf = tracer.shape
    size = clat // devices // chunks
    nlon = clon * devices
    half = nlon // 2
    order = sorted(range(1, devices), key=lambda off: -min(off, devices - off))
    peers = [lax.rem(me + off, devices) for off in order]
    west = lax.rem(me + devices - 1, devices)
    north, south = lax.rem(lat + bands - 1, bands), lax.rem(lat + 1, bands)

    loads = [
        pltpu.make_async_copy(table, place, table_sem.at[i])
        for i, (table, place) in enumerate(zip(tables, (even_h, even_l, odd_h, odd_l)))
    ]
    for copy in loads:
        copy.start()

    barrier = pltpu.get_barrier_semaphore()
    for peer in peers:
        pl.semaphore_signal(barrier, inc=1, device_id={"lon": peer}, device_id_type=MESH)
    for band in (north, south):
        pl.semaphore_signal(barrier, inc=1, device_id={"lat": band}, device_id_type=MESH)
    pl.semaphore_wait(barrier, devices + 1)

    def first(owner, c):
        flip = owner // (devices // 2)
        tile = owner * chunks + c + flip * (chunks - 1 - 2 * c)
        return pl.multiple_of(tile * size, size)

    def landing(c):
        return ring.at[c, pl.ds(2 + me * clon, clon)]

    def result(owner, c):
        return ring.at[c, pl.ds(owner * clon, clon + 4)]

    def home(c):
        return out.at[:, pl.ds(first(me, c), size), :]

    def source(owner, c):
        return tracer.at[:, pl.ds(first(owner, c), size), :]

    there, back = [], []
    for c in range(chunks):
        own = pltpu.make_async_copy(source(me, c), landing(c), self_a.at[c])
        sent = [
            pltpu.make_async_remote_copy(
                source(peer, c), landing(c), send_a.at[c, j], recv_a.at[c, j],
                device_id={"lon": peer}, device_id_type=MESH)
            for j, peer in enumerate(peers)
        ]
        own.start()
        for j, copy in enumerate(sent):
            if c:
                there[-1][1][j].wait_send()
            copy.start()
        there.append((own, sent))

    def edge(src, dst, k, device):
        return pltpu.make_async_remote_copy(
            src, dst, send_e.at[k], recv_e.at[k], device_id=device, device_id_type=MESH)

    def inner(ref, start):
        return ref.at[pl.ds(2, clon), pl.ds(start, 8), :]

    go_x = edge(courant.at[0, pl.ds(0, 1)], edge_x, 0, {"lon": west})
    go_y = edge(courant.at[1, :, pl.ds(0, 8), :], edge_y, 1, {"lat": north})
    go_north = edge(inner(out, 0), after, 2, {"lat": north})
    go_south = edge(inner(out, clat - 8), before, 3, {"lat": south})
    go_x.start()
    go_y.start()
    for copy in loads:
        copy.wait()

    lane = lax.broadcasted_iota(jnp.int32, (1, 2 * nf), 1)
    index = lax.broadcasted_iota(jnp.int32, (half, 2 * nf), 0)
    scale = 1.0 / nlon

    for c in range(chunks):
        own, sent = there[c]
        own.wait()
        for copy in sent:
            copy.wait_recv()
        flat = ring.at[c].reshape((nlon + 4) * size, nf)
        first_row = lat * clat + first(me, c)

        def pair(p, carry):
            def block(start, count, r):
                return (pl.ds(start * size + r, count, stride=size), slice(None))

            def load(start):
                return jnp.concatenate(
                    [flat[block(start, half, 2 * p + s)] for s in range(2)], axis=1)

            row = first_row + 2 * p
            cut = jnp.where(lane < nf, cut_ref[row], cut_ref[row + 1])
            mask = jnp.where(lane < nf, mask_ref[row], mask_ref[row + 1])
            low, high = load(2), load(2 + half)
            even = times(even_h, even_l, low + high)
            odd = times(odd_h, odd_l, low - high)
            wave = 2 * index
            even = jnp.where(jnp.minimum(wave, nlon - wave) < cut, even * scale, 0.0)
            odd = jnp.where(jnp.minimum(wave + 1, nlon - 1 - wave) < cut, odd * scale, 0.0)
            even = times(even_h, even_l, even)
            odd = times(odd_h, odd_l, odd)
            low = jnp.where(mask > 0, even + odd, low)
            high = jnp.where(mask > 0, even - odd, high)
            for s in range(2):
                r = 2 * p + s
                lo, hi = low[:, s * nf:(s + 1) * nf], high[:, s * nf:(s + 1) * nf]
                flat[block(2, half, r)] = lo
                flat[block(2 + half, half, r)] = hi
                for e in range(2):
                    flat[pl.ds((2 + nlon + e) * size + r, 1), :] = lo[e:e + 1]
                    flat[pl.ds(e * size + r, 1), :] = hi[half - 2 + e:half - 1 + e]
            return carry

        lax.fori_loop(0, size // 2, pair, 0)

        own = pltpu.make_async_copy(result(me, c), home(c), self_b.at[c])
        sent = [
            pltpu.make_async_remote_copy(
                result(peer, c), home(c), send_b.at[c, j], recv_b.at[c, j],
                device_id={"lon": peer}, device_id_type=MESH)
            for j, peer in enumerate(peers)
        ]
        own.start()
        for j, copy in enumerate(sent):
            if c + 1 < chunks:
                there[c + 1][1][j].wait_send()
            elif chunks == 1:
                there[c][1][j].wait_send()
            copy.start()
        back.append((own, sent))

    go_x.wait()
    for c in range(chunks):
        own, sent = back[c]
        own.wait()
        for copy in sent:
            copy.wait()
        if c == 0:
            @pl.when(lat > 0)
            def _():
                go_north.start()

            @pl.when(lat < bands - 1)
            def _():
                go_south.start()
    go_y.wait()

    @pl.when(lat > 0)
    def _():
        go_north.wait_send()
        go_south.wait_recv()

    @pl.when(lat < bands - 1)
    def _():
        go_south.wait_send()
        go_north.wait_recv()


def by_kernel(tracer, courant, polar_mask, cutoff, devices, bands):
    clon, clat, nf = tracer.shape
    nlon = clon * devices
    half = nlon // 2
    chunks = clat // devices // 8
    tables = [jnp.asarray(t) for t in hartley_tables(nlon)]
    smem = pl.BlockSpec(memory_space=pltpu.SMEM)
    hbm = pl.BlockSpec(memory_space=pltpu.HBM)
    dma = pltpu.SemaphoreType.DMA
    pairs, alone = dma((chunks, devices - 1)), dma((chunks,))
    shape = lambda *dims: jax.ShapeDtypeStruct(dims, jnp.float32)
    edge = shape(clon, 8, nf)
    return pl.pallas_call(
        functools.partial(filter_kernel, devices, bands, chunks),
        out_shape=(shape(clon + 4, clat, nf), edge, edge, shape(1, clat, nf), edge),
        in_specs=[smem, smem] + [hbm] * 6,
        out_specs=(hbm,) * 5,
        scratch_shapes=[pltpu.VMEM((chunks, nlon + 4, 8, nf), jnp.float32)]
        + [pltpu.VMEM((half, half), jnp.bfloat16)] * 4
        + [dma((4,)), pairs, pairs, alone, pairs, pairs, alone, dma((4,)), dma((4,))],
        compiler_params=pltpu.CompilerParams(
            collective_id=0, has_side_effects=True, vmem_limit_bytes=65000 << 10),
        name="filter_exchange",
    )(polar_mask, cutoff, tracer, courant, *tables)


def limited(far_low, low, high, far_high):
    face = (7.0 / 12.0) * (low + high) - (1.0 / 12.0) * (far_low + far_high)
    return jnp.minimum(jnp.maximum(face, jnp.minimum(low, high)), jnp.maximum(low, high))


def flux_kernel(bands, field, speed_x, next_x, edge_x, speed_y, edge_y, before, after, out, beyond,
                *scratch):
    count, clat = out.shape[0], out.shape[1]
    final = pl.program_id(0) == pl.num_programs(0) - 1
    talls, fluxes = scratch[:len(scratch) // 2], scratch[len(scratch) // 2:]
    lat = lax.axis_index("lat")
    top, bottom = lat > 0, lat < bands - 1

    def flux_x(i, speed):
        return speed * limited(field[i], field[i + 1], field[i + 2], field[i + 3])

    def column(c, low_flux, speed, tall, flux):
        high_flux = flux_x(c + 1, speed)
        value = field[c + 2]
        tall[8:8 + clat] = value
        tall[0:8] = jnp.where(top, before[c], 0.0)
        tall[8 + clat:16 + clat] = jnp.where(bottom, after[c], 0.0)
        flux[0:clat] = speed_y[c] * limited(
            tall[6:6 + clat], tall[7:7 + clat], value, tall[9:9 + clat])
        flux[clat:clat + 1] = jnp.where(bottom, edge_y[c, 0:1], 0.0) * limited(
            tall[6 + clat:7 + clat], tall[7 + clat:8 + clat],
            tall[8 + clat:9 + clat], tall[9 + clat:10 + clat])
        out[c] = value - (high_flux - low_flux) - (flux[1:clat + 1] - flux[0:clat])
        return high_flux

    beyond[...] = jnp.where(final, edge_x[0], next_x[0])
    group = len(talls)
    steps = count // group

    def columns(p, carry):
        for g in range(group):
            c = p * group + g
            speed = speed_x[jnp.minimum(c + 1, count - 1)]
            if g == group - 1:
                speed = jnp.where(p == steps - 1, beyond[...], speed)
            carry = column(c, carry, speed, talls[g], fluxes[g])
        return carry

    lax.fori_loop(0, steps, columns, flux_x(0, speed_x[0]))


def advect(field, before, after, edge_x, edge_y, courant, bands):
    _, clon, clat, nf = courant.shape
    block = math.gcd(clon, 16)
    group = math.gcd(block, 4)
    squeezed = pl.Squeezed()
    return pl.pallas_call(
        functools.partial(flux_kernel, bands),
        grid=(clon // block,),
        out_shape=jax.ShapeDtypeStruct((clon, clat, nf), jnp.float32),
        in_specs=[
            pl.BlockSpec((pl.Element(block + 4), pl.Element(clat), pl.Element(nf)),
                         lambda i: (i * block, 0, 0)),
            pl.BlockSpec((squeezed, block, clat, nf), lambda i: (0, i, 0, 0)),
            pl.BlockSpec((squeezed, 1, clat, nf),
                         lambda i: (0, jnp.minimum((i + 1) * block, clon - 1), 0, 0)),
            pl.BlockSpec((1, clat, nf), lambda i: (0, 0, 0)),
            pl.BlockSpec((squeezed, block, clat, nf), lambda i: (1, i, 0, 0)),
            pl.BlockSpec((block, 8, nf), lambda i: (i, 0, 0)),
            pl.BlockSpec((block, 8, nf), lambda i: (i, 0, 0)),
            pl.BlockSpec((block, 8, nf), lambda i: (i, 0, 0)),
        ],
        out_specs=pl.BlockSpec((block, clat, nf), lambda i: (i, 0, 0)),
        scratch_shapes=[pltpu.VMEM((clat, nf), jnp.float32)]
        + [pltpu.VMEM((clat + 16, nf), jnp.float32)] * group
        + [pltpu.VMEM((clat + 8, nf), jnp.float32)] * group,
        compiler_params=pltpu.CompilerParams(vmem_limit_bytes=65000 << 10),
        name="flux_step",
    )(field, courant, courant, edge_x, courant, edge_y, before, after)


def by_collectives(tracer, courant, polar_mask, cutoff, devices, bands):
    clon, clat, nf = tracer.shape
    nlon, half = clon * devices, clon * devices // 2
    circles = lax.all_to_all(tracer, "lon", split_axis=1, concat_axis=0, tiled=True)
    rows = clat // devices
    start = lax.axis_index("lat") * clat + lax.axis_index("lon") * rows
    mask = lax.dynamic_slice_in_dim(polar_mask, start, rows)[None, :, None]
    cut = lax.dynamic_slice_in_dim(cutoff, start, rows)[None, :, None]
    tables = [jnp.asarray(t).astype(jnp.float32) for t in hartley_tables(nlon)]
    apply = lambda h, l, x: jnp.einsum("uk,krc->urc", h + l, x, precision=lax.Precision.HIGHEST)
    low, high = circles[:half], circles[half:]
    wave = 2 * lax.broadcasted_iota(jnp.int32, (half, 1, 1), 0)
    even = apply(tables[0], tables[1], low + high) * (1.0 / nlon)
    odd = apply(tables[2], tables[3], low - high) * (1.0 / nlon)
    even = jnp.where(jnp.minimum(wave, nlon - wave) < cut, even, 0.0)
    odd = jnp.where(jnp.minimum(wave + 1, nlon - 1 - wave) < cut, odd, 0.0)
    even = apply(tables[0], tables[1], even)
    odd = apply(tables[2], tables[3], odd)
    smooth = jnp.concatenate([even + odd, even - odd], axis=0)
    done = jnp.where(mask > 0, smooth, circles)
    field = lax.all_to_all(done, "lon", split_axis=0, concat_axis=1, tiled=True)
    up = [(i, (i + 1) % devices) for i in range(devices)]
    down = [(j, i) for i, j in up]
    before = lax.ppermute(field[clon - 2:], "lon", up)
    after = lax.ppermute(field[:2], "lon", down)
    wide = jnp.concatenate([before, field, after], axis=0)
    south = [(i, i + 1) for i in range(bands - 1)]
    north = [(j, i) for i, j in south]
    edge_x = lax.ppermute(courant[0, :1], "lon", down)
    edge_y = lax.ppermute(courant[1, :, :8], "lat", north)
    before = lax.ppermute(field[:, clat - 8:], "lat", south)
    after = lax.ppermute(field[:, :8], "lat", north)
    return wide, before, after, edge_x, edge_y


def on_device(tracer, courant, polar_mask, cutoff):
    devices, bands = lax.axis_size("lon"), lax.axis_size("lat")
    fits = tracer.shape[1] % (8 * devices) == 0 and bands > 2
    build = by_kernel if fits else by_collectives
    parts = build(tracer, courant, polar_mask, cutoff, devices, bands)
    return advect(*parts, courant, bands)


def solution(mesh):
    return jax.shard_map(
        on_device,
        mesh=mesh,
        in_specs=(P("lon", "lat", None), P(None, "lon", "lat", None), P(), P()),
        out_specs=P("lon", "lat", None),
        check_vma=False,
    )
```

```python
import functools
import math

import jax
import jax.numpy as jnp
import ml_dtypes
import numpy as np
from jax import lax
from jax.experimental import pallas as pl
from jax.experimental.pallas import tpu as pltpu
from jax.sharding import PartitionSpec as P

MESH = pl.DeviceIdType.MESH


def halves(table):
    high = table.astype(ml_dtypes.bfloat16)
    low = (table - high.astype(np.float64)).astype(ml_dtypes.bfloat16)
    return high, low


def hartley_tables(nlon):
    half = nlon // 2
    u = np.arange(half, dtype=np.int64)
    even = (u[:, None] * u[None, :]) % half * (2.0 * math.pi / half)
    odd = ((2 * u[:, None] + 1) * (2 * u[None, :] + 1)) % (2 * nlon) * (math.pi / nlon)
    cas = lambda t: np.cos(t) + np.sin(t)
    return (*halves(cas(even)), *halves(cas(odd)))


def split(x):
    high = x.astype(jnp.bfloat16)
    return high, (x - high.astype(jnp.float32)).astype(jnp.bfloat16)


def times(high, low, x):
    x_high, x_low = split(x)
    dot = functools.partial(jnp.dot, preferred_element_type=jnp.float32)
    return dot(high[...], x_high) + (dot(low[...], x_high) + dot(high[...], x_low))


def filter_kernel(devices, bands, chunks, mask_ref, cut_ref, tracer, courant, *rest):
    tables, rest = rest[:4], rest[4:]
    (out, before, after, edge_x, edge_y, ring, even_h, even_l, odd_h, odd_l,
     table_sem, send_a, recv_a, self_a, send_b, recv_b, self_b, send_e, recv_e) = rest
    me, lat = lax.axis_index("lon"), lax.axis_index("lat")
    clon, clat, nf = tracer.shape
    size = clat // devices // chunks
    nlon = clon * devices
    half = nlon // 2
    order = sorted(range(1, devices), key=lambda off: -min(off, devices - off))
    peers = [lax.rem(me + off, devices) for off in order]
    west = lax.rem(me + devices - 1, devices)
    north, south = lax.rem(lat + bands - 1, bands), lax.rem(lat + 1, bands)

    loads = [
        pltpu.make_async_copy(table, place, table_sem.at[i])
        for i, (table, place) in enumerate(zip(tables, (even_h, even_l, odd_h, odd_l)))
    ]
    for copy in loads:
        copy.start()

    barrier = pltpu.get_barrier_semaphore()
    for peer in peers:
        pl.semaphore_signal(barrier, inc=1, device_id={"lon": peer}, device_id_type=MESH)
    for band in (north, south):
        pl.semaphore_signal(barrier, inc=1, device_id={"lat": band}, device_id_type=MESH)
    pl.semaphore_wait(barrier, devices + 1)

    def first(owner, c):
        flip = owner // (devices // 2)
        tile = owner * chunks + c + flip * (chunks - 1 - 2 * c)
        return pl.multiple_of(tile * size, size)

    def landing(c):
        return ring.at[c, pl.ds(2 + me * clon, clon)]

    def result(owner, c):
        return ring.at[c, pl.ds(owner * clon, clon + 4)]

    def home(c):
        return out.at[:, pl.ds(first(me, c), size), :]

    def source(owner, c):
        return tracer.at[:, pl.ds(first(owner, c), size), :]

    there, back = [], []
    for c in range(chunks):
        own = pltpu.make_async_copy(source(me, c), landing(c), self_a.at[c])
        sent = [
            pltpu.make_async_remote_copy(
                source(peer, c), landing(c), send_a.at[c, j], recv_a.at[c, j],
                device_id={"lon": peer}, device_id_type=MESH)
            for j, peer in enumerate(peers)
        ]
        own.start()
        for copy in sent:
            copy.start()
        there.append((own, sent))

    def edge(src, dst, k, device):
        return pltpu.make_async_remote_copy(
            src, dst, send_e.at[k], recv_e.at[k], device_id=device, device_id_type=MESH)

    def inner(ref, start):
        return ref.at[pl.ds(2, clon), pl.ds(start, 8), :]

    go_x = edge(courant.at[0, pl.ds(0, 1)], edge_x, 0, {"lon": west})
    go_y = edge(courant.at[1, :, pl.ds(0, 8), :], edge_y, 1, {"lat": north})
    go_north = edge(inner(out, 0), after, 2, {"lat": north})
    go_south = edge(inner(out, clat - 8), before, 3, {"lat": south})
    go_x.start()
    go_y.start()
    for copy in loads:
        copy.wait()

    lane = lax.broadcasted_iota(jnp.int32, (1, 2 * nf), 1)
    index = lax.broadcasted_iota(jnp.int32, (half, 2 * nf), 0)
    scale = 1.0 / nlon

    for c in range(chunks):
        own, sent = there[c]
        own.wait()
        for copy in sent:
            copy.wait_recv()
        flat = ring.at[c].reshape((nlon + 4) * size, nf)
        first_row = lat * clat + first(me, c)

        def pair(p, carry):
            def block(start, count, r):
                return (pl.ds(start * size + r, count, stride=size), slice(None))

            def load(start):
                return jnp.concatenate(
                    [flat[block(start, half, 2 * p + s)] for s in range(2)], axis=1)

            row = first_row + 2 * p
            cut = jnp.where(lane < nf, cut_ref[row], cut_ref[row + 1])
            mask = jnp.where(lane < nf, mask_ref[row], mask_ref[row + 1])
            low, high = load(2), load(2 + half)
            even = times(even_h, even_l, low + high)
            odd = times(odd_h, odd_l, low - high)
            wave = 2 * index
            even = jnp.where(jnp.minimum(wave, nlon - wave) < cut, even * scale, 0.0)
            odd = jnp.where(jnp.minimum(wave + 1, nlon - 1 - wave) < cut, odd * scale, 0.0)
            even = times(even_h, even_l, even)
            odd = times(odd_h, odd_l, odd)
            low = jnp.where(mask > 0, even + odd, low)
            high = jnp.where(mask > 0, even - odd, high)
            for s in range(2):
                r = 2 * p + s
                lo, hi = low[:, s * nf:(s + 1) * nf], high[:, s * nf:(s + 1) * nf]
                flat[block(2, half, r)] = lo
                flat[block(2 + half, half, r)] = hi
                for e in range(2):
                    flat[pl.ds((2 + nlon + e) * size + r, 1), :] = lo[e:e + 1]
                    flat[pl.ds(e * size + r, 1), :] = hi[half - 2 + e:half - 1 + e]
            return carry

        lax.fori_loop(0, size // 2, pair, 0)

        own = pltpu.make_async_copy(result(me, c), home(c), self_b.at[c])
        sent = [
            pltpu.make_async_remote_copy(
                result(peer, c), home(c), send_b.at[c, j], recv_b.at[c, j],
                device_id={"lon": peer}, device_id_type=MESH)
            for j, peer in enumerate(peers)
        ]
        own.start()
        for copy in sent:
            copy.start()
        back.append((own, sent))

    for own, sent in there:
        for copy in sent:
            copy.wait_send()
    go_x.wait()
    for c in range(chunks):
        own, sent = back[c]
        own.wait()
        for copy in sent:
            copy.wait()
        if c == 0:
            @pl.when(lat > 0)
            def _():
                go_north.start()

            @pl.when(lat < bands - 1)
            def _():
                go_south.start()
    go_y.wait()

    @pl.when(lat > 0)
    def _():
        go_north.wait_send()
        go_south.wait_recv()

    @pl.when(lat < bands - 1)
    def _():
        go_south.wait_send()
        go_north.wait_recv()


def by_kernel(tracer, courant, polar_mask, cutoff, devices, bands):
    clon, clat, nf = tracer.shape
    nlon = clon * devices
    half = nlon // 2
    chunks = clat // devices // 8
    tables = [jnp.asarray(t) for t in hartley_tables(nlon)]
    smem = pl.BlockSpec(memory_space=pltpu.SMEM)
    hbm = pl.BlockSpec(memory_space=pltpu.HBM)
    dma = pltpu.SemaphoreType.DMA
    pairs, alone = dma((chunks, devices - 1)), dma((chunks,))
    shape = lambda *dims: jax.ShapeDtypeStruct(dims, jnp.float32)
    edge = shape(clon, 8, nf)
    return pl.pallas_call(
        functools.partial(filter_kernel, devices, bands, chunks),
        out_shape=(shape(clon + 4, clat, nf), edge, edge, shape(1, clat, nf), edge),
        in_specs=[smem, smem] + [hbm] * 6,
        out_specs=(hbm,) * 5,
        scratch_shapes=[pltpu.VMEM((chunks, nlon + 4, 8, nf), jnp.float32)]
        + [pltpu.VMEM((half, half), jnp.bfloat16)] * 4
        + [dma((4,)), pairs, pairs, alone, pairs, pairs, alone, dma((4,)), dma((4,))],
        compiler_params=pltpu.CompilerParams(
            collective_id=0, has_side_effects=True, vmem_limit_bytes=65000 << 10),
        name="filter_exchange",
    )(polar_mask, cutoff, tracer, courant, *tables)


def limited(far_low, low, high, far_high):
    face = (7.0 / 12.0) * (low + high) - (1.0 / 12.0) * (far_low + far_high)
    return jnp.minimum(jnp.maximum(face, jnp.minimum(low, high)), jnp.maximum(low, high))


def flux_kernel(bands, field, speed_x, next_x, edge_x, speed_y, edge_y, before, after, out, tall, flux):
    count, clat = out.shape[0], out.shape[1]
    final = pl.program_id(0) == pl.num_programs(0) - 1
    lat = lax.axis_index("lat")
    top, bottom = lat > 0, lat < bands - 1

    def flux_x(i, speed):
        return speed * limited(field[i], field[i + 1], field[i + 2], field[i + 3])

    def column(c, low_flux, speed):
        high_flux = flux_x(c + 1, speed)
        value = field[c + 2]
        tall[8:8 + clat] = value
        tall[0:8] = jnp.where(top, before[c], 0.0)
        tall[8 + clat:16 + clat] = jnp.where(bottom, after[c], 0.0)
        flux[0:clat] = speed_y[c] * limited(
            tall[6:6 + clat], tall[7:7 + clat], value, tall[9:9 + clat])
        flux[clat:clat + 1] = jnp.where(bottom, edge_y[c, 0:1], 0.0) * limited(
            tall[6 + clat:7 + clat], tall[7 + clat:8 + clat],
            tall[8 + clat:9 + clat], tall[9 + clat:10 + clat])
        out[c] = value - (high_flux - low_flux) - (flux[1:clat + 1] - flux[0:clat])
        return high_flux

    carry = flux_x(0, speed_x[0])
    carry = lax.fori_loop(0, count - 1, lambda c, low: column(c, low, speed_x[c + 1]), carry)
    column(count - 1, carry, jnp.where(final, edge_x[0], next_x[0]))


def advect(field, before, after, edge_x, edge_y, courant, bands):
    _, clon, clat, nf = courant.shape
    block = math.gcd(clon, 16)
    squeezed = pl.Squeezed()
    return pl.pallas_call(
        functools.partial(flux_kernel, bands),
        grid=(clon // block,),
        out_shape=jax.ShapeDtypeStruct((clon, clat, nf), jnp.float32),
        in_specs=[
            pl.BlockSpec((pl.Element(block + 4), pl.Element(clat), pl.Element(nf)),
                         lambda i: (i * block, 0, 0)),
            pl.BlockSpec((squeezed, block, clat, nf), lambda i: (0, i, 0, 0)),
            pl.BlockSpec((squeezed, 1, clat, nf),
                         lambda i: (0, jnp.minimum((i + 1) * block, clon - 1), 0, 0)),
            pl.BlockSpec((1, clat, nf), lambda i: (0, 0, 0)),
            pl.BlockSpec((squeezed, block, clat, nf), lambda i: (1, i, 0, 0)),
            pl.BlockSpec((block, 8, nf), lambda i: (i, 0, 0)),
            pl.BlockSpec((block, 8, nf), lambda i: (i, 0, 0)),
            pl.BlockSpec((block, 8, nf), lambda i: (i, 0, 0)),
        ],
        out_specs=pl.BlockSpec((block, clat, nf), lambda i: (i, 0, 0)),
        scratch_shapes=[pltpu.VMEM((clat + 16, nf), jnp.float32),
                        pltpu.VMEM((clat + 8, nf), jnp.float32)],
        compiler_params=pltpu.CompilerParams(vmem_limit_bytes=65000 << 10),
        name="flux_step",
    )(field, courant, courant, edge_x, courant, edge_y, before, after)


def by_collectives(tracer, courant, polar_mask, cutoff, devices, bands):
    clon, clat, nf = tracer.shape
    nlon, half = clon * devices, clon * devices // 2
    circles = lax.all_to_all(tracer, "lon", split_axis=1, concat_axis=0, tiled=True)
    rows = clat // devices
    start = lax.axis_index("lat") * clat + lax.axis_index("lon") * rows
    mask = lax.dynamic_slice_in_dim(polar_mask, start, rows)[None, :, None]
    cut = lax.dynamic_slice_in_dim(cutoff, start, rows)[None, :, None]
    tables = [jnp.asarray(t).astype(jnp.float32) for t in hartley_tables(nlon)]
    apply = lambda h, l, x: jnp.einsum("uk,krc->urc", h + l, x, precision=lax.Precision.HIGHEST)
    low, high = circles[:half], circles[half:]
    wave = 2 * lax.broadcasted_iota(jnp.int32, (half, 1, 1), 0)
    even = apply(tables[0], tables[1], low + high) * (1.0 / nlon)
    odd = apply(tables[2], tables[3], low - high) * (1.0 / nlon)
    even = jnp.where(jnp.minimum(wave, nlon - wave) < cut, even, 0.0)
    odd = jnp.where(jnp.minimum(wave + 1, nlon - 1 - wave) < cut, odd, 0.0)
    even = apply(tables[0], tables[1], even)
    odd = apply(tables[2], tables[3], odd)
    smooth = jnp.concatenate([even + odd, even - odd], axis=0)
    done = jnp.where(mask > 0, smooth, circles)
    field = lax.all_to_all(done, "lon", split_axis=0, concat_axis=1, tiled=True)
    up = [(i, (i + 1) % devices) for i in range(devices)]
    down = [(j, i) for i, j in up]
    before = lax.ppermute(field[clon - 2:], "lon", up)
    after = lax.ppermute(field[:2], "lon", down)
    wide = jnp.concatenate([before, field, after], axis=0)
    south = [(i, i + 1) for i in range(bands - 1)]
    north = [(j, i) for i, j in south]
    edge_x = lax.ppermute(courant[0, :1], "lon", down)
    edge_y = lax.ppermute(courant[1, :, :8], "lat", north)
    before = lax.ppermute(field[:, clat - 8:], "lat", south)
    after = lax.ppermute(field[:, :8], "lat", north)
    return wide, before, after, edge_x, edge_y


def on_device(tracer, courant, polar_mask, cutoff):
    devices, bands = lax.axis_size("lon"), lax.axis_size("lat")
    fits = tracer.shape[1] % (8 * devices) == 0 and bands > 2
    build = by_kernel if fits else by_collectives
    parts = build(tracer, courant, polar_mask, cutoff, devices, bands)
    return advect(*parts, courant, bands)


def solution(mesh):
    return jax.shard_map(
        on_device,
        mesh=mesh,
        in_specs=(P("lon", "lat", None), P(None, "lon", "lat", None), P(), P()),
        out_specs=P("lon", "lat", None),
        check_vma=False,
    )
```
